32 devices in a mesh: image: 2 (over x), row: 16 (over z, y, core).
Axes of the slice: x: 2, y: 2, z: 4, core: 2. Of those that a mesh axis runs over, the one named last changes fastest.
Arguments:
- density: float32 [256, 7, 128, 128], P(('image', 'row')), parts along dimension 0, as said below
- block_columns: int32 [256, 7], P(('image', 'row')), parts along dimension 0, may hold values from -1 to 127, as said below
Outputs:
- purified: float32 [256, 7, 128, 128], P(('image', 'row')), parts along dimension 0
- occupation: float32 [6], P('image'), parts along dimension 0
The draws below stay inside these ranges and needn't reach their ends.
There are 2 independent parts, one for each index of `image`. The reference program is written for one: setup_inputs(seed, part) draws one part's arguments, and reference() takes and returns one part's arrays. A program takes and returns all parts, laid end to end along the dimension named above; each array names one. Nothing has to cross between parts.
Inputs may be any that keep to these rules, and one draw needn't show every extreme that they name: `block_columns`: slot s of block row i holds block column i - 3 + s or is empty (-1); slot 3 (column i) is never empty, and no slot points outside the matrix; the pattern is symmetric (j is in row i exactly when i is in row j); every draw has rows with all 7 slots filled. The density matrix is symmetric: the block in slot s of row i is the transpose of the block of row j = block_columns[i, s] whose column is i, and every diagonal block is symmetric.
All inputs are finite; a program needn't handle non-finite values.
Results may differ from the reference program's by a relative error of at most 0.0003.
Values sent between devices are 32-bit elements; how exact they have to be, the bound alone decides.
A program may use at most 128 MiB of HBM per device.

```python
import jax
import jax.numpy as jnp
from jax import lax

BS = 128
HALF = 3
STEPS = 2
K = 7
NB = 128
ORDER = 16384


def pattern(key):
    key_shift, key_roll = jax.random.split(key)
    shift = jax.random.randint(key_shift, (), 0, NB)
    row_ids = jnp.arange(NB, dtype=jnp.int32)
    chance = jnp.minimum(100, 25 + 100 * ((row_ids + shift) % NB) // NB)
    rolled = jax.random.randint(key_roll, (NB, HALF), 0, 100)
    offsets = jnp.arange(1, HALF + 1, dtype=jnp.int32)
    forward = (rolled < chance[:, None]) & (row_ids[:, None] + offsets[None, :] < NB)
    backward = []
    for offset in range(HALF, 0, -1):
        source = jnp.clip(row_ids - offset, 0, NB - 1)
        backward.append(jnp.where(row_ids - offset >= 0, forward[source, offset - 1], False))
    backward = jnp.stack(backward, 1)
    present = jnp.concatenate([backward, jnp.ones((NB, 1), dtype=bool), forward], 1)
    column_of = row_ids[:, None] + jnp.arange(-HALF, HALF + 1, dtype=jnp.int32)[None, :]
    return jnp.where(present, column_of, -1).astype(jnp.int32)


def symmetrize(jitter, columns):
    row_ids = jnp.arange(NB, dtype=jnp.int32)
    partners = []
    for slot in range(K):
        target = jnp.clip(row_ids - HALF + slot, 0, NB - 1).astype(jnp.int32)
        partners.append(jitter[target, K - 1 - slot])
    partner = jnp.stack(partners, 1)
    partner_t = jnp.swapaxes(partner, 2, 3)
    own_t = jnp.swapaxes(jitter, 2, 3)
    upper = (columns > row_ids[:, None]).astype(jnp.float32)[:, :, None, None]
    lower = ((columns < row_ids[:, None]) & (columns >= 0)).astype(jnp.float32)[:, :, None, None]
    diagonal = (columns == row_ids[:, None]).astype(jnp.float32)[:, :, None, None]
    return upper * jitter + lower * partner_t + diagonal * 0.5 * (jitter + own_t)


def draw_block_columns(key, part):
    return pattern(jax.random.fold_in(key, 7))


def draw_density(key, part):
    columns = pattern(jax.random.fold_in(key, 7))
    key_noise, key_diag = jax.random.split(jax.random.fold_in(key, 11))
    spread = 0.15 / (BS * K) ** 0.5
    jitter = jax.random.normal(key_noise, (NB, K, BS, BS), jnp.float32) * spread
    offset = jax.random.uniform(key_diag, (NB, BS), jnp.float32, -0.2, 0.2)
    jitter = symmetrize(jitter, columns)
    center = 0.25 + 0.5 * jnp.arange(NB, dtype=jnp.float32) / NB
    diagonal = center[:, None] + offset
    row_ids = jnp.arange(NB, dtype=jnp.int32)
    on_diagonal = (columns == row_ids[:, None]).astype(jnp.float32)
    identity = jnp.eye(BS, dtype=jnp.float32)
    blocks = jitter + on_diagonal[:, :, None, None] * (diagonal[:, None, :, None] * identity[None, None, :, :])
    return blocks * (columns >= 0).astype(jnp.float32)[:, :, None, None]


def setup_inputs(seed: int = 0, part: int = 0) -> dict:
    streams_of = jax.random.split(jax.random.key(seed), 3)
    own_keys = jax.random.split(jax.random.fold_in(streams_of[2], part), 3)
    density = draw_density(jax.random.fold_in(jax.random.fold_in(streams_of[2], part), 71), part)
    block_columns = draw_block_columns(jax.random.fold_in(jax.random.fold_in(streams_of[2], part), 71), part)
    return dict(density=density, block_columns=block_columns)


def pattern_product(first_rows, columns, second_rows):
    block_count = columns.shape[0]

    def one_row(packed):
        row_blocks, row_columns = packed
        present = row_columns >= 0
        where_rows = jnp.clip(row_columns, 0, block_count - 1).astype(jnp.int32)
        picked = second_rows[where_rows]
        picked_columns = columns[where_rows]
        matches = (picked_columns[None, :, :] == row_columns[:, None, None]) & present[:, None, None] & present[None, :, None]
        products = jnp.einsum('bxy,bsyz->bsxz', row_blocks, picked, precision=lax.Precision.HIGHEST)
        return jnp.einsum('abs,bsxz->axz', matches.astype(jnp.float32), products, precision=lax.Precision.HIGHEST)

    return lax.map(one_row, (first_rows, columns))


def full_trace(blocks, columns):
    row_ids = jnp.arange(columns.shape[0], dtype=jnp.int32)
    on_diagonal = (columns == row_ids[:, None]).astype(jnp.float32)
    return jnp.sum(on_diagonal * jnp.trace(blocks, axis1=2, axis2=3))


def reference(density, block_columns):
    present = (block_columns >= 0).astype(jnp.float32)
    current = density * present[:, :, None, None]
    traces = [full_trace(current, block_columns) / ORDER]
    for number in range(STEPS):
        square = pattern_product(current, block_columns, current)
        cube_term = pattern_product(square, block_columns, current)
        current = 3.0 * square - 2.0 * cube_term
        traces.append(full_trace(current, block_columns) / ORDER)
    return current, jnp.stack(traces)
```

```python
import functools

import jax
import jax.numpy as jnp
from jax import lax
from jax.experimental import pallas as pl
from jax.experimental.pallas import tpu as pltpu
from jax.sharding import PartitionSpec as P

STEPS = 2
MESH = pl.DeviceIdType.MESH


def split(x):
    hi = x.astype(jnp.bfloat16)
    return hi, (x - hi.astype(jnp.float32)).astype(jnp.bfloat16)


def dot(a, b):
    return jnp.dot(a, b, preferred_element_type=jnp.float32)


def kernel(n, dens, cols, out, occ, pf, qf, sf, left, cube_left, rq_hi, rq_lo, rz_hi, rz_lo, mask,
           low0, up0, low1, up1, tr, trs, send, recv, tsend, trecv):
    rows, slots, bs, _ = dens.shape
    pairs = rows // 2
    me = lax.axis_index("row")
    f32 = jnp.float32

    barrier = pltpu.get_barrier_semaphore()

    @pl.loop(1, n)
    def _(k):
        pl.semaphore_signal(barrier, inc=1, device_id={"row": lax.rem(me + k, n)}, device_id_type=MESH)

    def blk(i):
        return slice(i * bs, (i + 1) * bs)

    def put_right(p, rb, col, hi, lo):
        q = p + (col + 1) // 2
        row, half = 3 + rb - 2 * ((col - 1) // 2) + 2, (col - 1) % 2
        rq_hi[q, blk(row), blk(half)] = hi
        rq_lo[q, blk(row), blk(half)] = lo
        if col % 2 == 0 and 0 <= 3 + rb - col <= 3:
            z, row, half = p + 2 + col // 2, 3 + rb - col, 0
        elif col % 2 == 1 and 0 <= rb + 6 - col <= 3:
            z, row, half = p + 2 + (col - 7) // 2, rb + 6 - col, 1
        else:
            return
        rz_hi[z, blk(row), blk(half)] = hi
        rz_lo[z, blk(row), blk(half)] = lo

    def put_halo(j, c, x):
        hi, lo = split(x)
        q = (c - 1) // 2
        row = j - (2 * q - 2)
        if 0 <= row <= 7:
            rq_hi[q + 1, blk(row), blk((c - 1) % 2)] = hi
            rq_lo[q + 1, blk(row), blk((c - 1) % 2)] = lo
        if c % 2 == 0 and 0 <= j - c <= 3 and c < rows:
            rz_hi[c // 2 + 2, blk(j - c), blk(0)] = hi
            rz_lo[c // 2 + 2, blk(j - c), blk(0)] = lo
        if c % 2 == 1 and 0 <= j - (c - 3) <= 3 and 7 <= c < rows + 7:
            z = (c - 7) // 2 + 2
            rz_hi[z, blk(j - c + 3), blk(1)] = hi
            rz_lo[z, blk(j - c + 3), blk(1)] = lo

    def put_left(ref, p, rb, col, hi, lo):
        ref[p, blk(rb), blk(col)] = hi
        ref[p, blk(2 + rb), blk(col)] = lo

    rq_hi[...] = jnp.zeros_like(rq_hi)
    rq_lo[...] = jnp.zeros_like(rq_lo)
    rz_hi[...] = jnp.zeros_like(rz_hi)
    rz_lo[...] = jnp.zeros_like(rz_lo)
    mask[...] = jnp.zeros_like(mask)
    trs[...] = jnp.zeros_like(trs)
    eye = (lax.broadcasted_iota(jnp.int32, (bs, bs), 0) == lax.broadcasted_iota(jnp.int32, (bs, bs), 1)).astype(f32)

    def diag(x):
        return jnp.sum(x * eye, axis=0, keepdims=True)

    def load(p, total):
        zero = jnp.zeros((bs, bs), jnp.bfloat16)
        for rb in range(2):
            for s in range(slots):
                col = s + rb
                m = (cols[2 * p + rb, s] >= 0).astype(f32)
                mask[p, rb : rb + 1, blk(col)] = jnp.full((1, bs), 1.0, f32) * m
                x = dens[2 * p + rb, s] * m
                pf[p, blk(rb), blk(col)] = x
                hi, lo = split(x)
                put_left(left, p, rb, col, hi, lo)
                put_right(p, rb, col, hi, lo)
                if s == slots // 2:
                    total = total + diag(x)
            put_left(left, p, rb, 7 - 7 * rb, zero, zero)
        return total

    trs[0:1, :] = lax.fori_loop(0, pairs, load, jnp.zeros((1, bs), f32))

    pl.semaphore_wait(barrier, n - 1)
    top = rows + 3

    def halo_copies(src, low, up, first):
        nxt, prv = [], []
        for h in range(3):
            e = rows + h
            p, rb = divmod(e - 3, 2)
            c0, c1 = (e, rows + 3) if first else (rows, e + 4)
            nxt.append((src.at[p, blk(rb), pl.ds((c0 - 2 * p) * bs, (c1 - c0) * bs)], low[h]))
            e = 3 + h
            p, rb = divmod(e - 3, 2)
            c0, c1 = (e, 6) if first else (e - 3, 6)
            prv.append((src.at[p, blk(rb), pl.ds((c0 - 2 * p) * bs, (c1 - c0) * bs)], up[h]))
        base = 0 if first else 6

        def make(pairs_, off, dev):
            return [
                pltpu.make_async_remote_copy(
                    src_ref=s, dst_ref=d, send_sem=send.at[base + off + k], recv_sem=recv.at[base + off + k],
                    device_id={"row": dev}, device_id_type=MESH)
                for k, (s, d) in enumerate(pairs_)
            ]

        return make(nxt, 0, lax.rem(me + 1, n)), make(prv, 3, lax.rem(me + n - 1, n))

    def start(copies):
        nxt, prv = copies

        @pl.when(me < n - 1)
        def _():
            for c in nxt:
                c.start()

        @pl.when(me > 0)
        def _():
            for c in prv:
                c.start()

    def wait_sends(copies):
        nxt, prv = copies

        @pl.when(me < n - 1)
        def _():
            for c in nxt:
                c.wait_send()

        @pl.when(me > 0)
        def _():
            for c in prv:
                c.wait_send()

    first = halo_copies(pf, low0, up0, True)
    start(first)

    def own0(e, c):
        p, rb = divmod(e - 3, 2)
        return pf[p, blk(rb), blk(c - 2 * p)]

    for j in list(range(3)) + list(range(top, top + 3)):
        for c in range(max(3, j - 3), min(top, j + 4)):
            put_halo(j, c, own0(c, j).T)

    @pl.when(me > 0)
    def _():
        for h in range(3):
            first[0][h].wait_recv()
        for h in range(3):
            for c in range(h, 3):
                x = low0[h][:, blk(c - h)]
                put_halo(h, c, x)
                if c > h:
                    put_halo(c, h, x.T)

    @pl.when(me < n - 1)
    def _():
        for h in range(3):
            first[1][h].wait_recv()
        for h in range(3):
            for c in range(h, 3):
                x = up0[h][:, blk(c - h)]
                put_halo(top + h, top + c, x)
                if c > h:
                    put_halo(top + c, top + h, x.T)

    def groups(ref, p):
        for g, (k0, k1, b0) in enumerate(((0, 6, 2), (0, 8, 0), (2, 8, 0))):
            a = ref[p, :, k0 * bs : k1 * bs]
            b = slice(b0 * bs, (b0 + k1 - k0) * bs)
            y = dot(a, rq_hi[p + g + 1, b, :])
            y = y[: 2 * bs] + y[2 * bs :] + dot(a[: 2 * bs], rq_lo[p + g + 1, b, :])
            for rb in range(2):
                for h in range(2):
                    yield rb, 1 + 2 * g + h, y[blk(rb), blk(h)]
        a = jnp.concatenate([ref[p, blk(r), (r % 2) * 4 * bs : (r % 2 + 1) * 4 * bs] for r in range(4)], axis=0)
        y = dot(a, rz_hi[p + 2])
        y = y[: 2 * bs] + y[2 * bs :] + dot(a[: 2 * bs], rz_lo[p + 2])
        yield 0, 0, y[blk(0), blk(0)]
        yield 1, 7, y[blk(1), blk(1)]

    def square(p, carry):
        for rb, col, y in groups(left, p):
            y = y * mask[p, rb : rb + 1, blk(col)]
            sf[p, blk(rb), blk(col)] = y
            put_left(cube_left, p, rb, col, *split(y))
        return carry

    zero = jnp.zeros((bs, bs), jnp.bfloat16)
    for p in range(pairs):
        for rb in range(2):
            put_left(cube_left, p, rb, 7 - 7 * rb, zero, zero)

    lax.fori_loop(0, pairs, square, 0)

    def cube(p, total):
        for rb, col, y in groups(cube_left, p):
            x = 3.0 * sf[p, blk(rb), blk(col)] - 2.0 * (y * mask[p, rb : rb + 1, blk(col)])
            qf[p, blk(rb), blk(col)] = x
            put_left(left, p, rb, col, *split(x))
            if col == 3 + rb:
                total = total + diag(x)
        return total

    trs[1:2, :] = lax.fori_loop(0, pairs, cube, jnp.zeros((1, bs), f32))

    second = halo_copies(qf, low1, up1, False)
    start(second)

    def refill(p, carry):
        for rb in range(2):
            for s in range(slots):
                col = s + rb
                put_right(p, rb, col, left[p, blk(rb), blk(col)], left[p, blk(2 + rb), blk(col)])
        return carry

    lax.fori_loop(0, pairs, refill, 0)

    @pl.when(me > 0)
    def _():
        for h in range(3):
            second[0][h].wait_recv()
        for h in range(3):
            for c in range(h + 4):
                put_halo(h, c, low1[h][:, blk(c)])

    @pl.when(me < n - 1)
    def _():
        for h in range(3):
            second[1][h].wait_recv()
        for h in range(3):
            for c in range(rows + h, top + 3):
                put_halo(top + h, c, up1[h][:, blk(c - rows - h)])

    lax.fori_loop(0, pairs, square, 0)

    def last(p, total):
        for rb, col, y in groups(cube_left, p):
            x = 3.0 * sf[p, blk(rb), blk(col)] - 2.0 * (y * mask[p, rb : rb + 1, blk(col)])
            out[2 * p + rb, col - rb] = x
            if col == 3 + rb:
                total = total + diag(x)
        return total

    trs[2:3, :] = lax.fori_loop(0, pairs, last, jnp.zeros((1, bs), f32))

    def trace_copy(k):
        return pltpu.make_async_remote_copy(
            src_ref=trs, dst_ref=tr.at[me], send_sem=tsend.at[k], recv_sem=trecv.at[k],
            device_id={"row": lax.rem(me + k, n)}, device_id_type=MESH)

    wait_sends(first)
    wait_sends(second)

    @pl.loop(1, n)
    def _(k):
        trace_copy(k).start()

    tr[me] = trs[...]

    @pl.loop(1, n)
    def _(k):
        trace_copy(k).wait()

    total = lax.fori_loop(0, n, lambda k, t: t + tr[k], jnp.zeros((8, bs), f32))
    for k in range(STEPS + 1):
        occ[k] = jnp.sum(total[k : k + 1, :]) / (n * rows * bs)


def on_device(density, block_columns):
    rows, slots, bs, _ = density.shape
    n = lax.axis_size("row")
    pairs = rows // 2
    f32, bf16 = jnp.float32, jnp.bfloat16
    vm = pltpu.VMEM
    wide = 8 * bs
    return pl.pallas_call(
        functools.partial(kernel, n),
        out_shape=(jax.ShapeDtypeStruct(density.shape, f32), jax.ShapeDtypeStruct((STEPS + 1,), f32)),
        in_specs=[pl.BlockSpec(memory_space=pltpu.VMEM), pl.BlockSpec(memory_space=pltpu.SMEM)],
        out_specs=(pl.BlockSpec(memory_space=pltpu.VMEM), pl.BlockSpec(memory_space=pltpu.SMEM)),
        scratch_shapes=[
            vm((pairs, 2 * bs, wide), f32),
            vm((pairs, 2 * bs, wide), f32),
            vm((pairs, 2 * bs, wide), f32),
            vm((pairs, 4 * bs, wide), bf16),
            vm((pairs, 4 * bs, wide), bf16),
            vm((pairs + 4, wide, 2 * bs), bf16),
            vm((pairs + 4, wide, 2 * bs), bf16),
            vm((pairs + 4, 4 * bs, 2 * bs), bf16),
            vm((pairs + 4, 4 * bs, 2 * bs), bf16),
            vm((pairs, 8, wide), f32),
            [vm((bs, (3 - h) * bs), f32) for h in range(3)],
            [vm((bs, (3 - h) * bs), f32) for h in range(3)],
            [vm((bs, (4 + h) * bs), f32) for h in range(3)],
            [vm((bs, (6 - h) * bs), f32) for h in range(3)],
            vm((n, 8, bs), f32),
            vm((8, bs), f32),
            pltpu.SemaphoreType.DMA((12,)),
            pltpu.SemaphoreType.DMA((12,)),
            pltpu.SemaphoreType.DMA((n,)),
            pltpu.SemaphoreType.DMA((n,)),
        ],
        compiler_params=pltpu.CompilerParams(collective_id=0, has_side_effects=True, vmem_limit_bytes=60 << 20),
    )(density, block_columns)


def solution(mesh):
    in_specs = (P(("image", "row"), None, None, None), P(("image", "row"), None))
    out_specs = (P(("image", "row"), None, None, None), P("image"))
    return jax.shard_map(on_device, mesh=mesh, in_specs=in_specs, out_specs=out_specs, check_vma=False)
```

```python
import functools

import jax
import jax.numpy as jnp
from jax import lax
from jax.experimental import pallas as pl
from jax.experimental.pallas import tpu as pltpu
from jax.sharding import PartitionSpec as P

STEPS = 2
MESH = pl.DeviceIdType.MESH


def split(x):
    hi = x.astype(jnp.bfloat16)
    return hi, (x - hi.astype(jnp.float32)).astype(jnp.bfloat16)


def dot(a, b):
    return jnp.dot(a, b, preferred_element_type=jnp.float32)


def kernel(n, dens, cols, out, occ, pf, qf, sf, left, cube_left, rq_hi, rq_lo, rz_hi, rz_lo, mask,
           low0, up0, low1, up1, tr, trs, buf, send, recv, tsend, trecv, isem, osem):
    rows, slots, bs, _ = dens.shape
    pairs = rows // 2
    me = lax.axis_index("row")
    f32 = jnp.float32

    def fetch(p):
        return pltpu.make_async_copy(dens.at[pl.ds(2 * p, 2)], buf.at[pl.ds(2 * p, 2)], isem.at[p])

    for p in range(pairs):
        fetch(p).start()

    barrier = pltpu.get_barrier_semaphore()

    @pl.loop(1, n)
    def _(k):
        pl.semaphore_signal(barrier, inc=1, device_id={"row": lax.rem(me + k, n)}, device_id_type=MESH)

    def blk(i):
        return slice(i * bs, (i + 1) * bs)

    def put_right(p, rb, col, hi, lo):
        q = p + (col + 1) // 2
        row, half = 3 + rb - 2 * ((col - 1) // 2) + 2, (col - 1) % 2
        rq_hi[q, blk(row), blk(half)] = hi
        rq_lo[q, blk(row), blk(half)] = lo
        if col % 2 == 0 and 0 <= 3 + rb - col <= 3:
            z, row, half = p + 2 + col // 2, 3 + rb - col, 0
        elif col % 2 == 1 and 0 <= rb + 6 - col <= 3:
            z, row, half = p + 2 + (col - 7) // 2, rb + 6 - col, 1
        else:
            return
        rz_hi[z, blk(row), blk(half)] = hi
        rz_lo[z, blk(row), blk(half)] = lo

    def put_halo(j, c, x):
        hi, lo = split(x)
        q = (c - 1) // 2
        row = j - (2 * q - 2)
        if 0 <= row <= 7:
            rq_hi[q + 1, blk(row), blk((c - 1) % 2)] = hi
            rq_lo[q + 1, blk(row), blk((c - 1) % 2)] = lo
        if c % 2 == 0 and 0 <= j - c <= 3 and c < rows:
            rz_hi[c // 2 + 2, blk(j - c), blk(0)] = hi
            rz_lo[c // 2 + 2, blk(j - c), blk(0)] = lo
        if c % 2 == 1 and 0 <= j - (c - 3) <= 3 and 7 <= c < rows + 7:
            z = (c - 7) // 2 + 2
            rz_hi[z, blk(j - c + 3), blk(1)] = hi
            rz_lo[z, blk(j - c + 3), blk(1)] = lo

    def put_left(ref, p, rb, col, hi, lo):
        ref[p, blk(rb), blk(col)] = hi
        ref[p, blk(2 + rb), blk(col)] = lo

    rq_hi[...] = jnp.zeros_like(rq_hi)
    rq_lo[...] = jnp.zeros_like(rq_lo)
    rz_hi[...] = jnp.zeros_like(rz_hi)
    rz_lo[...] = jnp.zeros_like(rz_lo)
    mask[...] = jnp.zeros_like(mask)
    trs[...] = jnp.zeros_like(trs)
    eye = (lax.broadcasted_iota(jnp.int32, (bs, bs), 0) == lax.broadcasted_iota(jnp.int32, (bs, bs), 1)).astype(f32)

    def diag(x):
        return jnp.sum(x * eye, axis=0, keepdims=True)

    def load(p, total):
        zero = jnp.zeros((bs, bs), jnp.bfloat16)
        fetch(p).wait()
        for rb in range(2):
            for s in range(slots):
                col = s + rb
                m = (cols[2 * p + rb, s] >= 0).astype(f32)
                mask[p, rb : rb + 1, blk(col)] = jnp.full((1, bs), 1.0, f32) * m
                x = buf[2 * p + rb, s] * m
                pf[p, blk(rb), blk(col)] = x
                hi, lo = split(x)
                put_left(left, p, rb, col, hi, lo)
                put_right(p, rb, col, hi, lo)
                if s == slots // 2:
                    total = total + diag(x)
            put_left(left, p, rb, 7 - 7 * rb, zero, zero)
        return total

    trs[0:1, :] = lax.fori_loop(0, pairs, load, jnp.zeros((1, bs), f32))

    pl.semaphore_wait(barrier, n - 1)
    top = rows + 3

    def halo_copies(src, low, up, first):
        nxt, prv = [], []
        for h in range(3):
            e = rows + h
            p, rb = divmod(e - 3, 2)
            c0, c1 = (e, rows + 3) if first else (rows, e + 4)
            nxt.append((src.at[p, blk(rb), pl.ds((c0 - 2 * p) * bs, (c1 - c0) * bs)], low[h]))
            e = 3 + h
            p, rb = divmod(e - 3, 2)
            c0, c1 = (e, 6) if first else (e - 3, 6)
            prv.append((src.at[p, blk(rb), pl.ds((c0 - 2 * p) * bs, (c1 - c0) * bs)], up[h]))
        base = 0 if first else 6

        def make(pairs_, off, dev):
            return [
                pltpu.make_async_remote_copy(
                    src_ref=s, dst_ref=d, send_sem=send.at[base + off + k], recv_sem=recv.at[base + off + k],
                    device_id={"row": dev}, device_id_type=MESH)
                for k, (s, d) in enumerate(pairs_)
            ]

        return make(nxt, 0, lax.rem(me + 1, n)), make(prv, 3, lax.rem(me + n - 1, n))

    def start(copies):
        nxt, prv = copies

        @pl.when(me < n - 1)
        def _():
            for c in nxt:
                c.start()

        @pl.when(me > 0)
        def _():
            for c in prv:
                c.start()

    def wait_sends(copies):
        nxt, prv = copies

        @pl.when(me < n - 1)
        def _():
            for c in nxt:
                c.wait_send()

        @pl.when(me > 0)
        def _():
            for c in prv:
                c.wait_send()

    first = halo_copies(pf, low0, up0, True)
    start(first)

    def triple(a, b_hi, b_lo):
        y = dot(a, b_hi)
        return y[: 2 * bs] + y[2 * bs :] + dot(a[: 2 * bs], b_lo)

    spans = ((0, 6, 2), (0, 8, 0), (2, 8, 0))

    def part(ref, p, g, k0, k1):
        b0 = spans[g][2] - spans[g][0]
        b = slice((b0 + k0) * bs, (b0 + k1) * bs)
        return triple(ref[p, :, k0 * bs : k1 * bs], rq_hi[p + g + 1, b, :], rq_lo[p + g + 1, b, :])

    def blocks(g, y):
        for rb in range(2):
            for h in range(2):
                yield rb, 1 + 2 * g + h, y[blk(rb), blk(h)]

    def corners(ref, p):
        a = jnp.concatenate([ref[p, blk(r), (r % 2) * 4 * bs : (r % 2 + 1) * 4 * bs] for r in range(4)], axis=0)
        y = triple(a, rz_hi[p + 2], rz_lo[p + 2])
        yield 0, 0, y[blk(0), blk(0)]
        yield 1, 7, y[blk(1), blk(1)]

    def groups(ref, p, which=(0, 1, 2), corner=True):
        for g in which:
            yield from blocks(g, part(ref, p, g, *spans[g][:2]))
        if corner:
            yield from corners(ref, p)

    def inner(p):
        lo, hi = max(0, 3 - 2 * p), min(8, rows + 3 - 2 * p)
        return lo + lo % 2, hi - hi % 2

    def square_inner():
        for p in range(pairs):
            lo, hi = inner(p)
            for g in range(3):
                k0, k1 = max(lo, spans[g][0]), min(hi, spans[g][1])
                sf[p, :, (1 + 2 * g) * bs : (3 + 2 * g) * bs] = part(left, p, g, k0, k1)

    def square_outer():
        for p in range(pairs):
            lo, hi = inner(p)
            for g in range(3):
                y = sf[p, :, (1 + 2 * g) * bs : (3 + 2 * g) * bs]
                if lo > spans[g][0]:
                    y = y + part(left, p, g, spans[g][0], lo)
                if hi < spans[g][1]:
                    y = y + part(left, p, g, hi, spans[g][1])
                for rb, col, x in blocks(g, y):
                    put_square(p, rb, col, x)
            for rb, col, x in corners(left, p):
                put_square(p, rb, col, x)

    def put_square(p, rb, col, y):
        y = y * mask[p, rb : rb + 1, blk(col)]
        sf[p, blk(rb), blk(col)] = y
        put_left(cube_left, p, rb, col, *split(y))

    zero = jnp.zeros((bs, bs), jnp.bfloat16)
    for p in range(pairs):
        for rb in range(2):
            put_left(cube_left, p, rb, 7 - 7 * rb, zero, zero)

    square_inner()

    def own0(e, c):
        p, rb = divmod(e - 3, 2)
        return pf[p, blk(rb), blk(c - 2 * p)]

    for j in list(range(3)) + list(range(top, top + 3)):
        for c in range(max(3, j - 3), min(top, j + 4)):
            put_halo(j, c, own0(c, j).T)

    @pl.when(me > 0)
    def _():
        for h in range(3):
            first[0][h].wait_recv()
        for h in range(3):
            for c in range(h, 3):
                x = low0[h][:, blk(c - h)]
                put_halo(h, c, x)
                if c > h:
                    put_halo(c, h, x.T)

    @pl.when(me < n - 1)
    def _():
        for h in range(3):
            first[1][h].wait_recv()
        for h in range(3):
            for c in range(h, 3):
                x = up0[h][:, blk(c - h)]
                put_halo(top + h, top + c, x)
                if c > h:
                    put_halo(top + c, top + h, x.T)

    square_outer()

    def cube(p, total):
        for rb, col, y in groups(cube_left, p):
            x = 3.0 * sf[p, blk(rb), blk(col)] - 2.0 * (y * mask[p, rb : rb + 1, blk(col)])
            qf[p, blk(rb), blk(col)] = x
            put_left(left, p, rb, col, *split(x))
            if col == 3 + rb:
                total = total + diag(x)
        return total

    second = halo_copies(qf, low1, up1, False)
    traced = cube(pairs - 1, cube(0, jnp.zeros((1, bs), f32)))
    start((second[0][1:], second[1][:2]))
    trs[1:2, :] = lax.fori_loop(1, pairs - 1, cube, traced)

    def refill(p, carry):
        for rb in range(2):
            for s in range(slots):
                col = s + rb
                put_right(p, rb, col, left[p, blk(rb), blk(col)], left[p, blk(2 + rb), blk(col)])
        return carry

    lax.fori_loop(0, pairs, refill, 0)
    start((second[0][:1], second[1][2:]))
    square_inner()

    @pl.when(me > 0)
    def _():
        for h in range(3):
            second[0][h].wait_recv()
        for h in range(3):
            for c in range(h + 4):
                put_halo(h, c, low1[h][:, blk(c)])

    @pl.when(me < n - 1)
    def _():
        for h in range(3):
            second[1][h].wait_recv()
        for h in range(3):
            for c in range(rows + h, top + 3):
                put_halo(top + h, c, up1[h][:, blk(c - rows - h)])

    square_outer()

    def put_out(p, rb, col, y):
        x = 3.0 * sf[p, blk(rb), blk(col)] - 2.0 * (y * mask[p, rb : rb + 1, blk(col)])
        buf[2 * p + rb, col - rb] = x
        return x

    def last(p, total):
        for rb, col, y in groups(cube_left, p, (1,), False):
            x = put_out(p, rb, col, y)
            if col == 3 + rb:
                total = total + diag(x)
        return total

    trs[2:3, :] = lax.fori_loop(0, pairs, last, jnp.zeros((1, bs), f32))

    def rest(p, carry):
        for rb, col, y in groups(cube_left, p, (0, 2)):
            put_out(p, rb, col, y)
        return carry

    def trace_copy(k):
        return pltpu.make_async_remote_copy(
            src_ref=trs, dst_ref=tr.at[me], send_sem=tsend.at[k], recv_sem=trecv.at[k],
            device_id={"row": lax.rem(me + k, n)}, device_id_type=MESH)

    tr[me] = trs[...]
    wait_sends(first)
    wait_sends(second)

    @pl.loop(1, n)
    def _(k):
        trace_copy(k).start()

    def store(p):
        return pltpu.make_async_copy(buf.at[pl.ds(2 * p, 2)], out.at[pl.ds(2 * p, 2)], osem.at[p])

    for p in range(pairs):
        rest(p, 0)
        store(p).start()

    @pl.loop(1, n)
    def _(k):
        trace_copy(k).wait()

    total = lax.fori_loop(0, n, lambda k, t: t + tr[k], jnp.zeros((8, bs), f32))
    for k in range(STEPS + 1):
        occ[k] = jnp.sum(total[k : k + 1, :]) / (n * rows * bs)
    for p in range(pairs):
        store(p).wait()


def on_device(density, block_columns):
    rows, slots, bs, _ = density.shape
    n = lax.axis_size("row")
    pairs = rows // 2
    f32, bf16 = jnp.float32, jnp.bfloat16
    vm = pltpu.VMEM
    wide = 8 * bs
    return pl.pallas_call(
        functools.partial(kernel, n),
        out_shape=(jax.ShapeDtypeStruct(density.shape, f32), jax.ShapeDtypeStruct((STEPS + 1,), f32)),
        in_specs=[pl.BlockSpec(memory_space=pl.ANY), pl.BlockSpec(memory_space=pltpu.SMEM)],
        out_specs=(pl.BlockSpec(memory_space=pl.ANY), pl.BlockSpec(memory_space=pltpu.SMEM)),
        scratch_shapes=[
            vm((pairs, 2 * bs, wide), f32),
            vm((pairs, 2 * bs, wide), f32),
            vm((pairs, 2 * bs, wide), f32),
            vm((pairs, 4 * bs, wide), bf16),
            vm((pairs, 4 * bs, wide), bf16),
            vm((pairs + 4, wide, 2 * bs), bf16),
            vm((pairs + 4, wide, 2 * bs), bf16),
            vm((pairs + 4, 4 * bs, 2 * bs), bf16),
            vm((pairs + 4, 4 * bs, 2 * bs), bf16),
            vm((pairs, 8, wide), f32),
            [vm((bs, (3 - h) * bs), f32) for h in range(3)],
            [vm((bs, (3 - h) * bs), f32) for h in range(3)],
            [vm((bs, (4 + h) * bs), f32) for h in range(3)],
            [vm((bs, (6 - h) * bs), f32) for h in range(3)],
            vm((n, 8, bs), f32),
            vm((8, bs), f32),
            vm(density.shape, f32),
            pltpu.SemaphoreType.DMA((12,)),
            pltpu.SemaphoreType.DMA((12,)),
            pltpu.SemaphoreType.DMA((n,)),
            pltpu.SemaphoreType.DMA((n,)),
            pltpu.SemaphoreType.DMA((pairs,)),
            pltpu.SemaphoreType.DMA((pairs,)),
        ],
        compiler_params=pltpu.CompilerParams(collective_id=0, has_side_effects=True, vmem_limit_bytes=60 << 20),
    )(density, block_columns)


def solution(mesh):
    in_specs = (P(("image", "row"), None, None, None), P(("image", "row"), None))
    out_specs = (P(("image", "row"), None, None, None), P("image"))
    return jax.shard_map(on_device, mesh=mesh, in_specs=in_specs, out_specs=out_specs, check_vma=False)
```

```python
import functools

import jax
import jax.numpy as jnp
from jax import lax
from jax.experimental import pallas as pl
from jax.experimental.pallas import tpu as pltpu
from jax.sharding import PartitionSpec as P

STEPS = 2
MESH = pl.DeviceIdType.MESH


def split(x):
    hi = x.astype(jnp.bfloat16)
    return hi, (x - hi.astype(jnp.float32)).astype(jnp.bfloat16)


def dot(a, b):
    return jnp.dot(a, b, preferred_element_type=jnp.float32)


def kernel(n, dens, cols, out, occ, pf, qf, sf, left, cube_left, rq_hi, rq_lo, rz_hi, rz_lo, mask,
           low0, up0, low1, up1, s1, low2, up2, xl, xr_hi, xr_lo, tr, trs, buf, send, recv, tsend, trecv, isem, osem):
    rows, slots, bs, _ = dens.shape
    pairs = rows // 2
    me = lax.axis_index("row")
    f32 = jnp.float32

    def fetch(p):
        return pltpu.make_async_copy(dens.at[pl.ds(2 * p, 2)], buf.at[pl.ds(2 * p, 2)], isem.at[p])

    for p in range(pairs):
        fetch(p).start()

    barrier = pltpu.get_barrier_semaphore()

    @pl.loop(1, n)
    def _(k):
        pl.semaphore_signal(barrier, inc=1, device_id={"row": lax.rem(me + k, n)}, device_id_type=MESH)

    def blk(i):
        return slice(i * bs, (i + 1) * bs)

    def put_right(p, rb, col, hi, lo):
        q = p + (col + 1) // 2
        row, half = 3 + rb - 2 * ((col - 1) // 2) + 2, (col - 1) % 2
        rq_hi[q, blk(row), blk(half)] = hi
        rq_lo[q, blk(row), blk(half)] = lo
        if col % 2 == 0 and 0 <= 3 + rb - col <= 3:
            z, row, half = p + 2 + col // 2, 3 + rb - col, 0
        elif col % 2 == 1 and 0 <= rb + 6 - col <= 3:
            z, row, half = p + 2 + (col - 7) // 2, rb + 6 - col, 1
        else:
            return
        rz_hi[z, blk(row), blk(half)] = hi
        rz_lo[z, blk(row), blk(half)] = lo

    def put_halo(j, c, x):
        hi, lo = split(x)
        q = (c - 1) // 2
        row = j - (2 * q - 2)
        if 0 <= row <= 7:
            rq_hi[q + 1, blk(row), blk((c - 1) % 2)] = hi
            rq_lo[q + 1, blk(row), blk((c - 1) % 2)] = lo
        if c % 2 == 0 and 0 <= j - c <= 3 and c < rows:
            rz_hi[c // 2 + 2, blk(j - c), blk(0)] = hi
            rz_lo[c // 2 + 2, blk(j - c), blk(0)] = lo
        if c % 2 == 1 and 0 <= j - (c - 3) <= 3 and 7 <= c < rows + 7:
            z = (c - 7) // 2 + 2
            rz_hi[z, blk(j - c + 3), blk(1)] = hi
            rz_lo[z, blk(j - c + 3), blk(1)] = lo

    def put_left(ref, p, rb, col, hi, lo):
        ref[p, blk(rb), blk(col)] = hi
        ref[p, blk(2 + rb), blk(col)] = lo

    mask[...] = jnp.zeros_like(mask)
    trs[...] = jnp.zeros_like(trs)
    eye = (lax.broadcasted_iota(jnp.int32, (bs, bs), 0) == lax.broadcasted_iota(jnp.int32, (bs, bs), 1)).astype(f32)

    def diag(x):
        return jnp.sum(x * eye, axis=0, keepdims=True)

    def load(p, total):
        fetch(p).wait()
        for rb in range(2):
            for s in range(slots):
                col = s + rb
                m = (cols[2 * p + rb, s] >= 0).astype(f32)
                mask[p, rb : rb + 1, blk(col)] = jnp.full((1, bs), 1.0, f32) * m
                x = buf[2 * p + rb, s] * m
                pf[p, blk(rb), blk(col)] = x
                if s == slots // 2:
                    total = total + diag(x)
        return total

    def fill(p, carry):
        zero = jnp.zeros((bs, bs), jnp.bfloat16)
        for rb in range(2):
            for s in range(slots):
                col = s + rb
                hi, lo = split(pf[p, blk(rb), blk(col)])
                put_left(left, p, rb, col, hi, lo)
                put_right(p, rb, col, hi, lo)
            put_left(left, p, rb, 7 - 7 * rb, zero, zero)
        return carry

    trs[0:1, :] = lax.fori_loop(0, pairs, load, jnp.zeros((1, bs), f32))

    pl.semaphore_wait(barrier, n - 1)
    top = rows + 3

    def halo_copies(src, low, up, triangle, base):
        nxt, prv = [], []
        for h in range(3):
            e = rows + h
            p, rb = divmod(e - 3, 2)
            c0, c1 = (e if triangle else rows), rows + 3
            nxt.append((src.at[p, blk(rb), pl.ds((c0 - 2 * p) * bs, (c1 - c0) * bs)], low[h]))
            e = 3 + h
            p, rb = divmod(e - 3, 2)
            c0, c1 = (e if triangle else 3), 6
            prv.append((src.at[p, blk(rb), pl.ds((c0 - 2 * p) * bs, (c1 - c0) * bs)], up[h]))

        def make(pairs_, off, dev):
            return [
                pltpu.make_async_remote_copy(
                    src_ref=s, dst_ref=d, send_sem=send.at[base + off + k], recv_sem=recv.at[base + off + k],
                    device_id={"row": dev}, device_id_type=MESH)
                for k, (s, d) in enumerate(pairs_)
            ]

        return make(nxt, 0, lax.rem(me + 1, n)), make(prv, 3, lax.rem(me + n - 1, n))

    def start(copies):
        nxt, prv = copies

        @pl.when(me < n - 1)
        def _():
            for c in nxt:
                c.start()

        @pl.when(me > 0)
        def _():
            for c in prv:
                c.start()

    def wait_sends(copies):
        nxt, prv = copies

        @pl.when(me < n - 1)
        def _():
            for c in nxt:
                c.wait_send()

        @pl.when(me > 0)
        def _():
            for c in prv:
                c.wait_send()

    first = halo_copies(pf, low0, up0, True, 0)
    start(first)

    rq_hi[...] = jnp.zeros_like(rq_hi)
    rq_lo[...] = jnp.zeros_like(rq_lo)
    rz_hi[...] = jnp.zeros_like(rz_hi)
    rz_lo[...] = jnp.zeros_like(rz_lo)
    lax.fori_loop(0, pairs, fill, 0)


    def triple(a, b_hi, b_lo):
        y = dot(a, b_hi)
        return y[: 2 * bs] + y[2 * bs :] + dot(a[: 2 * bs], b_lo)

    spans = ((0, 6, 2), (0, 8, 0), (2, 8, 0))

    def part(ref, p, g, k0, k1):
        b0 = spans[g][2] - spans[g][0]
        b = slice((b0 + k0) * bs, (b0 + k1) * bs)
        return triple(ref[p, :, k0 * bs : k1 * bs], rq_hi[p + g + 1, b, :], rq_lo[p + g + 1, b, :])

    def blocks(g, y):
        for rb in range(2):
            for h in range(2):
                yield rb, 1 + 2 * g + h, y[blk(rb), blk(h)]

    def corners(ref, p):
        a = jnp.concatenate([ref[p, blk(r), (r % 2) * 4 * bs : (r % 2 + 1) * 4 * bs] for r in range(4)], axis=0)
        y = triple(a, rz_hi[p + 2], rz_lo[p + 2])
        yield 0, 0, y[blk(0), blk(0)]
        yield 1, 7, y[blk(1), blk(1)]

    def groups(ref, p, which=(0, 1, 2), corner=True):
        for g in which:
            yield from blocks(g, part(ref, p, g, *spans[g][:2]))
        if corner:
            yield from corners(ref, p)

    def inner(p):
        lo, hi = max(0, 3 - 2 * p), min(8, rows + 3 - 2 * p)
        return lo + lo % 2, hi - hi % 2

    def square_inner(sf):
        for p in range(pairs):
            lo, hi = inner(p)
            for g in range(3):
                k0, k1 = max(lo, spans[g][0]), min(hi, spans[g][1])
                sf[p, :, (1 + 2 * g) * bs : (3 + 2 * g) * bs] = part(left, p, g, k0, k1)

    def square_outer(sf, order):
        for p in order:
            lo, hi = inner(p)
            for g in range(3):
                y = sf[p, :, (1 + 2 * g) * bs : (3 + 2 * g) * bs]
                if lo > spans[g][0]:
                    y = y + part(left, p, g, spans[g][0], lo)
                if hi < spans[g][1]:
                    y = y + part(left, p, g, hi, spans[g][1])
                for rb, col, x in blocks(g, y):
                    put_square(sf, p, rb, col, x)
            for rb, col, x in corners(left, p):
                put_square(sf, p, rb, col, x)

    def put_square(sf, p, rb, col, y):
        y = y * mask[p, rb : rb + 1, blk(col)]
        sf[p, blk(rb), blk(col)] = y
        put_left(cube_left, p, rb, col, *split(y))

    zero = jnp.zeros((bs, bs), jnp.bfloat16)
    for p in range(pairs):
        for rb in range(2):
            put_left(cube_left, p, rb, 7 - 7 * rb, zero, zero)

    square_inner(s1)

    def own0(e, c):
        p, rb = divmod(e - 3, 2)
        return pf[p, blk(rb), blk(c - 2 * p)]

    for j in list(range(3)) + list(range(top, top + 3)):
        for c in range(max(3, j - 3), min(top, j + 4)):
            put_halo(j, c, own0(c, j).T)

    @pl.when(me > 0)
    def _():
        for h in range(3):
            first[0][h].wait_recv()
        for h in range(3):
            for c in range(h, 3):
                x = low0[h][:, blk(c - h)]
                put_halo(h, c, x)
                if c > h:
                    put_halo(c, h, x.T)

    @pl.when(me < n - 1)
    def _():
        for h in range(3):
            first[1][h].wait_recv()
        for h in range(3):
            for c in range(h, 3):
                x = up0[h][:, blk(c - h)]
                put_halo(top + h, top + c, x)
                if c > h:
                    put_halo(top + c, top + h, x.T)

    mid = halo_copies(s1, low2, up2, True, 12)
    square_outer(s1, (0, pairs - 1))
    start((mid[0][1:], mid[1][:2]))
    square_outer(s1, range(1, pairs - 1))
    start((mid[0][:1], mid[1][2:]))

    def cube(p, total):
        for rb, col, y in groups(cube_left, p):
            x = 3.0 * s1[p, blk(rb), blk(col)] - 2.0 * (y * mask[p, rb : rb + 1, blk(col)])
            qf[p, blk(rb), blk(col)] = x
            put_left(left, p, rb, col, *split(x))
            if col == 3 + rb:
                total = total + diag(x)
        return total

    second = halo_copies(qf, low1, up1, False, 6)
    traced = cube(pairs - 1, cube(0, jnp.zeros((1, bs), f32)))
    start((second[0][1:], second[1][:2]))
    trs[1:2, :] = lax.fori_loop(1, pairs - 1, cube, traced)

    def refill(p, carry):
        for rb in range(2):
            for s in range(slots):
                col = s + rb
                put_right(p, rb, col, left[p, blk(rb), blk(col)], left[p, blk(2 + rb), blk(col)])
        return carry

    lax.fori_loop(0, pairs, refill, 0)
    start((second[0][:1], second[1][2:]))
    square_inner(sf)

    def cross(low):
        own = [3, 4, 5] if low else [rows, rows + 1, rows + 2]
        far = [0, 1, 2] if low else [top, top + 1, top + 2]
        ks = far + own if low else own + far
        copies, got = (mid[0], low2) if low else (mid[1], up2)
        for h in range(3):
            copies[h].wait_recv()
        for i, k in enumerate(ks):
            for h, j in enumerate(far):
                if k in far:
                    r, c = min(far.index(k), h), max(far.index(k), h)
                    x = got[r][:, blk(c - r)]
                    x = x if far.index(k) <= h else x.T
                elif abs(k - j) <= 3:
                    x = s1[(k - 3) // 2, blk((k - 3) % 2), blk(j - 2 * ((k - 3) // 2))]
                else:
                    x = jnp.zeros((bs, bs), f32)
                xr_hi[blk(i), blk(h)], xr_lo[blk(i), blk(h)] = split(x)
            for h, c in enumerate(own):
                if abs(k - c) <= 3:
                    x = pf[(c - 3) // 2, blk((c - 3) % 2), blk(k - 2 * ((c - 3) // 2))]
                else:
                    x = jnp.zeros((bs, bs), f32)
                xl[blk(h), blk(i)], xl[blk(3 + h), blk(i)] = split(x)
        y = dot(xl[...], xr_hi[...])
        y = y[: 3 * bs] + y[3 * bs :] + dot(xl[: 3 * bs], xr_lo[...])
        for i, c in enumerate(own):
            p, rb = divmod(c - 3, 2)
            for h, j in enumerate(far):
                if abs(c - j) <= 3:
                    col = j - 2 * p
                    x = 3.0 * s1[p, blk(rb), blk(col)] - 2.0 * (y[blk(i), blk(h)] * mask[p, rb : rb + 1, blk(col)])
                    put_halo(j, c, x.T)

    @pl.when(me > 0)
    def _():
        cross(True)

    @pl.when(me < n - 1)
    def _():
        cross(False)

    @pl.when(me > 0)
    def _():
        for h in range(3):
            second[0][h].wait_recv()
        for h in range(3):
            for c in range(3):
                put_halo(h, c, low1[h][:, blk(c)])

    @pl.when(me < n - 1)
    def _():
        for h in range(3):
            second[1][h].wait_recv()
        for h in range(3):
            for c in range(3):
                put_halo(top + h, top + c, up1[h][:, blk(c)])

    square_outer(sf, range(pairs))

    def put_out(p, rb, col, y):
        x = 3.0 * sf[p, blk(rb), blk(col)] - 2.0 * (y * mask[p, rb : rb + 1, blk(col)])
        buf[2 * p + rb, col - rb] = x
        return x

    def last(p, total):
        for rb, col, y in groups(cube_left, p, (1,), False):
            x = put_out(p, rb, col, y)
            if col == 3 + rb:
                total = total + diag(x)
        return total

    trs[2:3, :] = lax.fori_loop(0, pairs, last, jnp.zeros((1, bs), f32))

    def rest(p, carry):
        for rb, col, y in groups(cube_left, p, (0, 2)):
            put_out(p, rb, col, y)
        return carry

    def trace_copy(k):
        return pltpu.make_async_remote_copy(
            src_ref=trs, dst_ref=tr.at[me], send_sem=tsend.at[k], recv_sem=trecv.at[k],
            device_id={"row": lax.rem(me + k, n)}, device_id_type=MESH)

    tr[me] = trs[...]
    wait_sends(first)
    wait_sends(mid)
    wait_sends(second)

    @pl.loop(1, n)
    def _(k):
        trace_copy(k).start()

    def store(p):
        return pltpu.make_async_copy(buf.at[pl.ds(2 * p, 2)], out.at[pl.ds(2 * p, 2)], osem.at[p])

    for p in range(pairs):
        rest(p, 0)
        store(p).start()

    @pl.loop(1, n)
    def _(k):
        trace_copy(k).wait()

    total = lax.fori_loop(0, n, lambda k, t: t + tr[k], jnp.zeros((8, bs), f32))
    for k in range(STEPS + 1):
        occ[k] = jnp.sum(total[k : k + 1, :]) / (n * rows * bs)
    for p in range(pairs):
        store(p).wait()


def on_device(density, block_columns):
    rows, slots, bs, _ = density.shape
    n = lax.axis_size("row")
    pairs = rows // 2
    f32, bf16 = jnp.float32, jnp.bfloat16
    vm = pltpu.VMEM
    wide = 8 * bs
    return pl.pallas_call(
        functools.partial(kernel, n),
        out_shape=(jax.ShapeDtypeStruct(density.shape, f32), jax.ShapeDtypeStruct((STEPS + 1,), f32)),
        in_specs=[pl.BlockSpec(memory_space=pl.ANY), pl.BlockSpec(memory_space=pltpu.SMEM)],
        out_specs=(pl.BlockSpec(memory_space=pl.ANY), pl.BlockSpec(memory_space=pltpu.SMEM)),
        scratch_shapes=[
            vm((pairs, 2 * bs, wide), f32),
            vm((pairs, 2 * bs, wide), f32),
            vm((pairs, 2 * bs, wide), f32),
            vm((pairs, 4 * bs, wide), bf16),
            vm((pairs, 4 * bs, wide), bf16),
            vm((pairs + 4, wide, 2 * bs), bf16),
            vm((pairs + 4, wide, 2 * bs), bf16),
            vm((pairs + 4, 4 * bs, 2 * bs), bf16),
            vm((pairs + 4, 4 * bs, 2 * bs), bf16),
            vm((pairs, 8, wide), f32),
            [vm((bs, (3 - h) * bs), f32) for h in range(3)],
            [vm((bs, (3 - h) * bs), f32) for h in range(3)],
            [vm((bs, 3 * bs), f32) for h in range(3)],
            [vm((bs, 3 * bs), f32) for h in range(3)],
            vm((pairs, 2 * bs, wide), f32),
            [vm((bs, (3 - h) * bs), f32) for h in range(3)],
            [vm((bs, (3 - h) * bs), f32) for h in range(3)],
            vm((6 * bs, 6 * bs), bf16),
            vm((6 * bs, 3 * bs), bf16),
            vm((6 * bs, 3 * bs), bf16),
            vm((n, 8, bs), f32),
            vm((8, bs), f32),
            vm(density.shape, f32),
            pltpu.SemaphoreType.DMA((18,)),
            pltpu.SemaphoreType.DMA((18,)),
            pltpu.SemaphoreType.DMA((n,)),
            pltpu.SemaphoreType.DMA((n,)),
            pltpu.SemaphoreType.DMA((pairs,)),
            pltpu.SemaphoreType.DMA((pairs,)),
        ],
        compiler_params=pltpu.CompilerParams(collective_id=0, has_side_effects=True, vmem_limit_bytes=60 << 20),
    )(density, block_columns)


def solution(mesh):
    in_specs = (P(("image", "row"), None, None, None), P(("image", "row"), None))
    out_specs = (P(("image", "row"), None, None, None), P("image"))
    return jax.shard_map(on_device, mesh=mesh, in_specs=in_specs, out_specs=out_specs, check_vma=False)
```

```python
import functools

import jax
import jax.numpy as jnp
from jax import lax
from jax.experimental import pallas as pl
from jax.experimental.pallas import tpu as pltpu
from jax.sharding import PartitionSpec as P

STEPS = 2
MESH = pl.DeviceIdType.MESH


def split(x):
    hi = x.astype(jnp.bfloat16)
    return hi, (x - hi.astype(jnp.float32)).astype(jnp.bfloat16)


def dot(a, b):
    return jnp.dot(a, b, preferred_element_type=jnp.float32)


def kernel(n, dens, cols, out, occ, pf, qf, sf, left, cube_left, rq_hi, rq_lo, rz_hi, rz_lo, mask,
           low0, up0, low1, up1, s1, low2, up2, xl, xr_hi, xr_lo, tr, trs, buf, send, recv, tsend, trecv, isem, osem):
    rows, slots, bs, _ = dens.shape
    pairs = rows // 2
    me = lax.axis_index("row")
    f32 = jnp.float32

    def fetch(p):
        return pltpu.make_async_copy(dens.at[pl.ds(2 * p, 2)], buf.at[pl.ds(2 * p, 2)], isem.at[p])

    for p in range(pairs):
        fetch(p).start()

    barrier = pltpu.get_barrier_semaphore()

    @pl.loop(1, n)
    def _(k):
        pl.semaphore_signal(barrier, inc=1, device_id={"row": lax.rem(me + k, n)}, device_id_type=MESH)

    def blk(i):
        return slice(i * bs, (i + 1) * bs)

    def put_right(p, rb, col, hi, lo):
        q = p + (col + 1) // 2
        row, half = 3 + rb - 2 * ((col - 1) // 2) + 2, (col - 1) % 2
        rq_hi[q, blk(row), blk(half)] = hi
        rq_lo[q, blk(row), blk(half)] = lo
        if col % 2 == 0 and 0 <= 3 + rb - col <= 3:
            z, row, half = p + 2 + col // 2, 3 + rb - col, 0
        elif col % 2 == 1 and 0 <= rb + 6 - col <= 3:
            z, row, half = p + 2 + (col - 7) // 2, rb + 6 - col, 1
        else:
            return
        rz_hi[z, blk(row), blk(half)] = hi
        rz_lo[z, blk(row), blk(half)] = lo

    def put_halo(j, c, x):
        hi, lo = split(x)
        q = (c - 1) // 2
        row = j - (2 * q - 2)
        if 0 <= row <= 7:
            rq_hi[q + 1, blk(row), blk((c - 1) % 2)] = hi
            rq_lo[q + 1, blk(row), blk((c - 1) % 2)] = lo
        if c % 2 == 0 and 0 <= j - c <= 3 and c < rows:
            rz_hi[c // 2 + 2, blk(j - c), blk(0)] = hi
            rz_lo[c // 2 + 2, blk(j - c), blk(0)] = lo
        if c % 2 == 1 and 0 <= j - (c - 3) <= 3 and 7 <= c < rows + 7:
            z = (c - 7) // 2 + 2
            rz_hi[z, blk(j - c + 3), blk(1)] = hi
            rz_lo[z, blk(j - c + 3), blk(1)] = lo

    def put_left(ref, p, rb, col, hi, lo):
        ref[p, blk(rb), blk(col)] = hi
        ref[p, blk(2 + rb), blk(col)] = lo

    mask[...] = jnp.zeros_like(mask)
    trs[...] = jnp.zeros_like(trs)
    eye = (lax.broadcasted_iota(jnp.int32, (bs, bs), 0) == lax.broadcasted_iota(jnp.int32, (bs, bs), 1)).astype(f32)

    def diag(x):
        return jnp.sum(x * eye, axis=0, keepdims=True)

    def load(p, total):
        fetch(p).wait()
        for rb in range(2):
            for s in range(slots):
                col = s + rb
                m = (cols[2 * p + rb, s] >= 0).astype(f32)
                mask[p, rb : rb + 1, blk(col)] = jnp.full((1, bs), 1.0, f32) * m
                x = buf[2 * p + rb, s] * m
                pf[p, blk(rb), blk(col)] = x
                if s == slots // 2:
                    total = total + diag(x)
        return total

    def fill(p, carry):
        zero = jnp.zeros((bs, bs), jnp.bfloat16)
        for rb in range(2):
            for s in range(slots):
                col = s + rb
                hi, lo = split(pf[p, blk(rb), blk(col)])
                put_left(left, p, rb, col, hi, lo)
                put_right(p, rb, col, hi, lo)
            put_left(left, p, rb, 7 - 7 * rb, zero, zero)
        return carry

    trs[0:1, :] = lax.fori_loop(0, pairs, load, jnp.zeros((1, bs), f32))

    pl.semaphore_wait(barrier, n - 1)
    top = rows + 3

    def halo_copies(src, low, up, triangle, base):
        nxt, prv = [], []
        for h in range(3):
            e = rows + h
            p, rb = divmod(e - 3, 2)
            c0, c1 = (e if triangle else rows), rows + 3
            nxt.append((src.at[p, blk(rb), pl.ds((c0 - 2 * p) * bs, (c1 - c0) * bs)], low[h]))
            e = 3 + h
            p, rb = divmod(e - 3, 2)
            c0, c1 = (e if triangle else 3), 6
            prv.append((src.at[p, blk(rb), pl.ds((c0 - 2 * p) * bs, (c1 - c0) * bs)], up[h]))

        def make(pairs_, off, dev):
            return [
                pltpu.make_async_remote_copy(
                    src_ref=s, dst_ref=d, send_sem=send.at[base + off + k], recv_sem=recv.at[base + off + k],
                    device_id={"row": dev}, device_id_type=MESH)
                for k, (s, d) in enumerate(pairs_)
            ]

        return make(nxt, 0, lax.rem(me + 1, n)), make(prv, 3, lax.rem(me + n - 1, n))

    def start(copies):
        nxt, prv = copies

        @pl.when(me < n - 1)
        def _():
            for c in nxt:
                c.start()

        @pl.when(me > 0)
        def _():
            for c in prv:
                c.start()

    def wait_sends(copies):
        nxt, prv = copies

        @pl.when(me < n - 1)
        def _():
            for c in nxt:
                c.wait_send()

        @pl.when(me > 0)
        def _():
            for c in prv:
                c.wait_send()

    first = halo_copies(pf, low0, up0, True, 0)
    start(first)

    rq_hi[...] = jnp.zeros_like(rq_hi)
    rq_lo[...] = jnp.zeros_like(rq_lo)
    rz_hi[...] = jnp.zeros_like(rz_hi)
    rz_lo[...] = jnp.zeros_like(rz_lo)
    lax.fori_loop(0, pairs, fill, 0)


    def triple(a, b_hi, b_lo):
        y = dot(a, b_hi)
        return y[: 2 * bs] + y[2 * bs :] + dot(a[: 2 * bs], b_lo)

    spans = ((0, 6, 2), (0, 8, 0), (2, 8, 0))

    def part(ref, p, g, k0, k1):
        b0 = spans[g][2] - spans[g][0]
        b = slice((b0 + k0) * bs, (b0 + k1) * bs)
        return triple(ref[p, :, k0 * bs : k1 * bs], rq_hi[p + g + 1, b, :], rq_lo[p + g + 1, b, :])

    def blocks(g, y):
        for rb in range(2):
            for h in range(2):
                yield rb, 1 + 2 * g + h, y[blk(rb), blk(h)]

    def corners(ref, p):
        a = jnp.concatenate([ref[p, blk(r), (r % 2) * 4 * bs : (r % 2 + 1) * 4 * bs] for r in range(4)], axis=0)
        y = triple(a, rz_hi[p + 2], rz_lo[p + 2])
        yield 0, 0, y[blk(0), blk(0)]
        yield 1, 7, y[blk(1), blk(1)]

    def groups(ref, p, which=(0, 1, 2), corner=True):
        for g in which:
            yield from blocks(g, part(ref, p, g, *spans[g][:2]))
        if corner:
            yield from corners(ref, p)

    def inner(p):
        lo, hi = max(0, 3 - 2 * p), min(8, rows + 3 - 2 * p)
        return lo + lo % 2, hi - hi % 2

    def square_inner(sf):
        for p in range(pairs):
            lo, hi = inner(p)
            for g in range(3):
                k0, k1 = max(lo, spans[g][0]), min(hi, spans[g][1])
                sf[p, :, (1 + 2 * g) * bs : (3 + 2 * g) * bs] = part(left, p, g, k0, k1)

    def square_outer(sf, order):
        for p in order:
            lo, hi = inner(p)
            for g in range(3):
                y = sf[p, :, (1 + 2 * g) * bs : (3 + 2 * g) * bs]
                if lo > spans[g][0]:
                    y = y + part(left, p, g, spans[g][0], lo)
                if hi < spans[g][1]:
                    y = y + part(left, p, g, hi, spans[g][1])
                for rb, col, x in blocks(g, y):
                    put_square(sf, p, rb, col, x)
            for rb, col, x in corners(left, p):
                put_square(sf, p, rb, col, x)

    def put_square(sf, p, rb, col, y):
        y = y * mask[p, rb : rb + 1, blk(col)]
        sf[p, blk(rb), blk(col)] = y
        put_left(cube_left, p, rb, col, *split(y))

    zero = jnp.zeros((bs, bs), jnp.bfloat16)
    for p in range(pairs):
        for rb in range(2):
            put_left(cube_left, p, rb, 7 - 7 * rb, zero, zero)

    square_inner(s1)

    def own0(e, c):
        p, rb = divmod(e - 3, 2)
        return pf[p, blk(rb), blk(c - 2 * p)]

    for j in list(range(3)) + list(range(top, top + 3)):
        for c in range(max(3, j - 3), min(top, j + 4)):
            put_halo(j, c, own0(c, j).T)

    @pl.when(me > 0)
    def _():
        for h in range(3):
            first[0][h].wait_recv()
        for h in range(3):
            for c in range(h, 3):
                x = low0[h][:, blk(c - h)]
                put_halo(h, c, x)
                if c > h:
                    put_halo(c, h, x.T)

    @pl.when(me < n - 1)
    def _():
        for h in range(3):
            first[1][h].wait_recv()
        for h in range(3):
            for c in range(h, 3):
                x = up0[h][:, blk(c - h)]
                put_halo(top + h, top + c, x)
                if c > h:
                    put_halo(top + c, top + h, x.T)

    mid = halo_copies(s1, low2, up2, True, 12)
    square_outer(s1, (0, pairs - 1))
    start((mid[0][1:], mid[1][:2]))
    square_outer(s1, range(1, pairs - 1))
    start((mid[0][:1], mid[1][2:]))

    def cube(p, total):
        for rb, col, y in groups(cube_left, p):
            x = 3.0 * s1[p, blk(rb), blk(col)] - 2.0 * (y * mask[p, rb : rb + 1, blk(col)])
            qf[p, blk(rb), blk(col)] = x
            put_left(left, p, rb, col, *split(x))
            if col == 3 + rb:
                total = total + diag(x)
        return total

    second = halo_copies(qf, low1, up1, False, 6)
    traced = cube(pairs - 1, cube(0, jnp.zeros((1, bs), f32)))
    start((second[0][1:], second[1][:2]))
    trs[1:2, :] = lax.fori_loop(1, pairs - 1, cube, traced)

    def refill(p, carry):
        for rb in range(2):
            for s in range(slots):
                col = s + rb
                put_right(p, rb, col, left[p, blk(rb), blk(col)], left[p, blk(2 + rb), blk(col)])
        return carry

    lax.fori_loop(0, pairs, refill, 0)
    start((second[0][:1], second[1][2:]))
    square_inner(sf)

    def cross(low):
        own = [3, 4, 5] if low else [rows, rows + 1, rows + 2]
        far = [0, 1, 2] if low else [top, top + 1, top + 2]
        ks = far + own if low else own + far
        copies, got = (mid[0], low2) if low else (mid[1], up2)
        for h in range(3):
            copies[h].wait_recv()
        for i, k in enumerate(ks):
            for h, j in enumerate(far):
                if k in far:
                    r, c = min(far.index(k), h), max(far.index(k), h)
                    x = got[r][:, blk(c - r)]
                    x = x if far.index(k) <= h else x.T
                elif abs(k - j) <= 3:
                    x = s1[(k - 3) // 2, blk((k - 3) % 2), blk(j - 2 * ((k - 3) // 2))]
                else:
                    x = jnp.zeros((bs, bs), f32)
                xr_hi[blk(i), blk(h)], xr_lo[blk(i), blk(h)] = split(x)
            for h, c in enumerate(own):
                if abs(k - c) <= 3:
                    x = pf[(c - 3) // 2, blk((c - 3) % 2), blk(k - 2 * ((c - 3) // 2))]
                else:
                    x = jnp.zeros((bs, bs), f32)
                xl[blk(h), blk(i)], xl[blk(3 + h), blk(i)] = split(x)
        y = dot(xl[...], xr_hi[...])
        y = y[: 3 * bs] + y[3 * bs :] + dot(xl[: 3 * bs], xr_lo[...])
        for i, c in enumerate(own):
            p, rb = divmod(c - 3, 2)
            for h, j in enumerate(far):
                if abs(c - j) <= 3:
                    col = j - 2 * p
                    x = 3.0 * s1[p, blk(rb), blk(col)] - 2.0 * (y[blk(i), blk(h)] * mask[p, rb : rb + 1, blk(col)])
                    put_halo(j, c, x.T)

    def side(low):
        @pl.when(me > 0 if low else me < n - 1)
        def _():
            cross(low)
            copies, got, first_row = (second[0], low1, 0) if low else (second[1], up1, top)
            for h in range(3):
                copies[h].wait_recv()
            for h in range(3):
                for c in range(3):
                    put_halo(first_row + h, first_row + c, got[h][:, blk(c)])

        square_outer(sf, range(pairs // 2) if low else range(pairs // 2, pairs))

    def put_out(p, rb, col, y):
        x = 3.0 * sf[p, blk(rb), blk(col)] - 2.0 * (y * mask[p, rb : rb + 1, blk(col)])
        buf[2 * p + rb, col - rb] = x
        return x

    def last(p, total):
        for rb, col, y in groups(cube_left, p, (1,), False):
            x = put_out(p, rb, col, y)
            if col == 3 + rb:
                total = total + diag(x)
        return total

    def rest(p, carry):
        for rb, col, y in groups(cube_left, p, (0, 2)):
            put_out(p, rb, col, y)
        return carry

    def store(p):
        return pltpu.make_async_copy(buf.at[pl.ds(2 * p, 2)], out.at[pl.ds(2 * p, 2)], osem.at[p])

    def finish(low_first):
        half = pairs // 2
        a, b = ((0, half), (half, pairs)) if low_first else ((half, pairs), (0, half))
        side(low_first)
        total = lax.fori_loop(*a, last, jnp.zeros((1, bs), f32))
        for p in range(*a):
            rest(p, 0)
            store(p).start()
        side(not low_first)
        trs[2:3, :] = lax.fori_loop(*b, last, total)

    odd = lax.rem(me, 2)

    @pl.when(odd == 0)
    def _():
        finish(False)

    @pl.when(odd == 1)
    def _():
        finish(True)

    def trace_copy(k):
        return pltpu.make_async_remote_copy(
            src_ref=trs, dst_ref=tr.at[me], send_sem=tsend.at[k], recv_sem=trecv.at[k],
            device_id={"row": lax.rem(me + k, n)}, device_id_type=MESH)

    tr[me] = trs[...]
    wait_sends(first)
    wait_sends(mid)
    wait_sends(second)

    @pl.loop(1, n)
    def _(k):
        trace_copy(k).start()

    for i in range(pairs // 2):
        p = odd * (pairs // 2) + i
        rest(p, 0)
        store(p).start()

    @pl.loop(1, n)
    def _(k):
        trace_copy(k).wait()

    total = lax.fori_loop(0, n, lambda k, t: t + tr[k], jnp.zeros((8, bs), f32))
    for k in range(STEPS + 1):
        occ[k] = jnp.sum(total[k : k + 1, :]) / (n * rows * bs)
    for p in range(pairs):
        store(p).wait()


def on_device(density, block_columns):
    rows, slots, bs, _ = density.shape
    n = lax.axis_size("row")
    pairs = rows // 2
    f32, bf16 = jnp.float32, jnp.bfloat16
    vm = pltpu.VMEM
    wide = 8 * bs
    return pl.pallas_call(
        functools.partial(kernel, n),
        out_shape=(jax.ShapeDtypeStruct(density.shape, f32), jax.ShapeDtypeStruct((STEPS + 1,), f32)),
        in_specs=[pl.BlockSpec(memory_space=pl.ANY), pl.BlockSpec(memory_space=pltpu.SMEM)],
        out_specs=(pl.BlockSpec(memory_space=pl.ANY), pl.BlockSpec(memory_space=pltpu.SMEM)),
        scratch_shapes=[
            vm((pairs, 2 * bs, wide), f32),
            vm((pairs, 2 * bs, wide), f32),
            vm((pairs, 2 * bs, wide), f32),
            vm((pairs, 4 * bs, wide), bf16),
            vm((pairs, 4 * bs, wide), bf16),
            vm((pairs + 4, wide, 2 * bs), bf16),
            vm((pairs + 4, wide, 2 * bs), bf16),
            vm((pairs + 4, 4 * bs, 2 * bs), bf16),
            vm((pairs + 4, 4 * bs, 2 * bs), bf16),
            vm((pairs, 8, wide), f32),
            [vm((bs, (3 - h) * bs), f32) for h in range(3)],
            [vm((bs, (3 - h) * bs), f32) for h in range(3)],
            [vm((bs, 3 * bs), f32) for h in range(3)],
            [vm((bs, 3 * bs), f32) for h in range(3)],
            vm((pairs, 2 * bs, wide), f32),
            [vm((bs, (3 - h) * bs), f32) for h in range(3)],
            [vm((bs, (3 - h) * bs), f32) for h in range(3)],
            vm((6 * bs, 6 * bs), bf16),
            vm((6 * bs, 3 * bs), bf16),
            vm((6 * bs, 3 * bs), bf16),
            vm((n, 8, bs), f32),
            vm((8, bs), f32),
            vm(density.shape, f32),
            pltpu.SemaphoreType.DMA((18,)),
            pltpu.SemaphoreType.DMA((18,)),
            pltpu.SemaphoreType.DMA((n,)),
            pltpu.SemaphoreType.DMA((n,)),
            pltpu.SemaphoreType.DMA((pairs,)),
            pltpu.SemaphoreType.DMA((pairs,)),
        ],
        compiler_params=pltpu.CompilerParams(collective_id=0, has_side_effects=True, vmem_limit_bytes=60 << 20),
    )(density, block_columns)


def solution(mesh):
    in_specs = (P(("image", "row"), None, None, None), P(("image", "row"), None))
    out_specs = (P(("image", "row"), None, None, None), P("image"))
    return jax.shard_map(on_device, mesh=mesh, in_specs=in_specs, out_specs=out_specs, check_vma=False)
```
